32 devices in a mesh: shard: 4 (over z), ctx: 4 (over x, core), tp: 2 (over y).
Axes of the slice: x: 2, y: 2, z: 4, core: 2. Of those that a mesh axis runs over, the one named last changes fastest.
Arguments:
- inputs: bfloat16 [4, 4096, 768], P('shard', 'ctx'), may hold values from -6 to 6
- teacher: bfloat16 [4, 4096, 768], P('shard', 'ctx'), may hold values from -6 to 6
- segments: int32 [4, 4096], P('shard', 'ctx'), may hold values from 0 to 7, never falling along the last dimension, each value on 1 to 2048 neighbouring positions
- valid_mask: int32 [4, 4096], P('shard', 'ctx'), may hold values from 0 to 1, as said below
- offsets: int32 [12], P('tp'), may hold values from 0 to 1, as said below
- first_gain: bfloat16 [768], P('shard'), may hold values from 0.5 to 1.5
- first_shift: bfloat16 [768], P('shard'), may hold values from -1.25 to 1.25
- query_weight: bfloat16 [768, 768], P('shard', 'tp'), may hold values from -0.21875 to 0.21875
- key_weight: bfloat16 [768, 768], P('shard', 'tp'), may hold values from -0.21875 to 0.21875
- value_weight: bfloat16 [768, 768], P('shard', 'tp'), may hold values from -0.21875 to 0.21875
- query_bias: bfloat16 [12, 64], P('tp', 'shard'), may hold values from -1.75 to 1.75
- value_bias: bfloat16 [12, 64], P('tp', 'shard'), may hold values from -1.75 to 1.75
- mixed_gain: bfloat16 [12, 64], P('tp', 'shard'), may hold values from 0.5 to 1.5
- mixed_shift: bfloat16 [12, 64], P('tp', 'shard'), may hold values from -1.25 to 1.25
- output_weight: bfloat16 [768, 768], P('tp', 'shard'), may hold values from -0.21875 to 0.21875
- output_bias: bfloat16 [768], P('shard'), may hold values from -1.25 to 1.25
- second_gain: bfloat16 [768], P('shard'), may hold values from 0.5 to 1.5
- second_shift: bfloat16 [768], P('shard'), may hold values from -1.25 to 1.25
- inner_weight: bfloat16 [768, 3072], P('shard', 'tp'), may hold values from -0.21875 to 0.21875
- inner_bias: bfloat16 [24, 128], P('tp', 'shard'), may hold values from -3 to 3
- hidden_gain: bfloat16 [24, 128], P('tp', 'shard'), may hold values from 0.5 to 1.5
- hidden_shift: bfloat16 [24, 128], P('tp', 'shard'), may hold values from -1.25 to 1.25
- outer_weight: bfloat16 [3072, 768], P('tp', 'shard'), may hold values from -0.109375 to 0.109375
- outer_bias: bfloat16 [768], P('shard'), may hold values from -1.25 to 1.25
Outputs:
- result: bfloat16 [4, 4096, 768], P('shard', 'ctx')
- loss: float32 [], replicated
- input_grad: float32 [4, 4096, 768], P('shard', 'ctx')
- first_gain_grad: float32 [768], P('shard')
- first_shift_grad: float32 [768], P('shard')
- query_weight_grad: float32 [768, 768], P('shard', 'tp')
- key_weight_grad: float32 [768, 768], P('shard', 'tp')
- value_weight_grad: float32 [768, 768], P('shard', 'tp')
- query_bias_grad: float32 [12, 64], P('tp', 'shard')
- value_bias_grad: float32 [12, 64], P('tp', 'shard')
- mixed_gain_grad: float32 [12, 64], P('tp', 'shard')
- mixed_shift_grad: float32 [12, 64], P('tp', 'shard')
- output_weight_grad: float32 [768, 768], P('tp', 'shard')
- output_bias_grad: float32 [768], P('shard')
- second_gain_grad: float32 [768], P('shard')
- second_shift_grad: float32 [768], P('shard')
- inner_weight_grad: float32 [768, 3072], P('shard', 'tp')
- inner_bias_grad: float32 [24, 128], P('tp', 'shard')
- hidden_gain_grad: float32 [24, 128], P('tp', 'shard')
- hidden_shift_grad: float32 [24, 128], P('tp', 'shard')
- outer_weight_grad: float32 [3072, 768], P('tp', 'shard')
- outer_bias_grad: float32 [768], P('shard')
The draws below stay inside these ranges and needn't reach their ends.
Inputs may be any that keep to these rules, and one draw needn't show every extreme that they name: `valid_mask`: in every sequence the valid tokens form a prefix of 1024 tokens or more. `segments`: document numbers never fall along a sequence. Both offsets occur among the heads.
All inputs are finite; a program needn't handle non-finite values.
Results may differ from the reference program's by a relative error of at most 0.012.
Values may be sent and summed in bfloat16 or wider, within the bound.
No kernel may reach another device: no remote copies, remote signals or barrier semaphores. Data moves between devices by JAX's collectives and lax.ppermute only.
A program may use at most 192 MiB of HBM per device.

```python
import math
import jax
import jax.numpy as jnp
import numpy as np
from jax import lax

D = 768
H = 12
HD = 64
FF = 3072
SEQ = 4096
SEG = 2048
SEQS = 4
TOKENS = 16384


def draw_valid_mask(key, part):
    lengths = jax.random.randint(key, (SEQS,), SEQ // 4, SEQ + 1)
    positions = jnp.arange(SEQ, dtype=jnp.int32)
    return (positions[None, :] < lengths[:, None]).astype(jnp.int32)


def draw_offsets(key, part):
    bits_key = jax.random.fold_in(key, 11)
    order_key = jax.random.fold_in(key, 23)
    chosen = jax.random.randint(bits_key, (H,), 0, 2).astype(jnp.int32)
    order = jax.random.permutation(order_key, H).astype(jnp.int32)
    index = jnp.arange(H, dtype=jnp.int32)
    chosen = jnp.where(index == order[0], jnp.int32(0), chosen)
    chosen = jnp.where(index == order[1], jnp.int32(1), chosen)
    return chosen.astype(jnp.int32)


def block_scale(stream_key, shape, cuts, smallest, largest):
    def one(position, parts):
        heights = jax.random.uniform(jax.random.fold_in(jax.random.fold_in(stream_key, 6), position), (parts,), jnp.float32, smallest / len(cuts), largest / len(cuts))
        return jnp.repeat(jnp.exp(heights), shape[position] // parts).reshape((-1,) + (1,) * (len(shape) - position - 1))

    factor_of = one(*cuts[0])
    for cut in cuts[1:]:
        factor_of = factor_of * one(*cut)
    return factor_of


def split_up(amount, total, limit, skew):
    portions = [(1 << 20) // math.isqrt(grade ** skew) + 1 for grade in range(2, amount + 1)]
    rest, given = total - limit - (amount - 1), [1] * (amount - 1)
    while rest > 0:
        movable = [i for i in range(amount - 1) if given[i] < limit]
        mass, budget = sum([portions[i] for i in movable]), rest
        for i in movable:
            addition = min(limit - given[i], max(1, budget * portions[i] // mass), rest)
            given[i] = given[i] + addition
            rest = rest - addition
    return np.array([limit] + given)


def uneven(rng, count, total, limit, skew):
    if count == 2:
        one = jax.random.randint(rng, (), max(1, total - limit), min(limit, total - 1) + 1)
        return jnp.stack([one, total - one])
    sizes = jnp.asarray(split_up(count, total, limit, skew), jnp.int32)
    couples = (count - 1) // 2
    source_of, receiver = sizes[1:1 + 2 * couples:2], sizes[2:2 + 2 * couples:2]
    slack = jnp.minimum(source_of - 1, limit - receiver)
    shifted = jax.random.randint(jax.random.fold_in(rng, 1), (couples,), 0, 1 << 20) % (slack + 1)
    sizes = sizes.at[1:1 + 2 * couples:2].set(source_of - shifted).at[2:2 + 2 * couples:2].set(receiver + shifted)
    return sizes[jax.random.permutation(jax.random.fold_in(rng, 2), count)]


def normal_values(key, dims, deviation, most, cuts=(), kind=jnp.bfloat16):
    loudness = block_scale(key, dims, cuts, -0.22, 0.18) if cuts else 1.0
    result = jax.random.normal(key, dims, jnp.float32) * deviation * loudness
    return jnp.minimum(jnp.maximum(result, -most), most).astype(kind)


def setup_inputs(seed: int = 0) -> dict:
    streams_of = jax.random.split(jax.random.key(seed), 25)
    inputs = normal_values(streams_of[0], (SEQS, SEQ, D), 1.0, 6.0, ((0, 4), (1, 4)))
    teacher = normal_values(streams_of[1], (SEQS, SEQ, D), 1.0, 6.0, ((0, 4), (1, 4)))
    segments = jax.vmap(lambda own: jnp.searchsorted(jnp.cumsum(uneven(own, max(SEQ // 512, 4), SEQ, SEQ // 2, 0)), jnp.arange(SEQ), side="right"))(jax.random.split(streams_of[2], SEQS)).reshape((SEQS, SEQ)).astype(jnp.int32)
    valid_mask = draw_valid_mask(jax.random.fold_in(streams_of[24], 71), 0)
    offsets = draw_offsets(jax.random.fold_in(streams_of[24], 71), 0)
    first_gain = jnp.clip(1.0 + 0.1 * jax.random.normal(streams_of[5], (D,), jnp.float32), 0.5, 1.5).astype(jnp.bfloat16)
    first_shift = normal_values(streams_of[6], (D,), 0.2, 1.25, ((0, 4),))
    query_weight = normal_values(streams_of[7], (D, D), D ** -0.5, 0.21875, ((0, 4), (1, 2)))
    key_weight = normal_values(streams_of[8], (D, D), D ** -0.5, 0.21875, ((0, 4), (1, 2)))
    value_weight = normal_values(streams_of[9], (D, D), D ** -0.5, 0.21875, ((0, 4), (1, 2)))
    query_bias = normal_values(streams_of[10], (H, HD), 0.3, 1.75, ((0, 2), (1, 4)))
    value_bias = normal_values(streams_of[11], (H, HD), 0.3, 1.75, ((0, 2), (1, 4)))
    mixed_gain = jnp.clip(1.0 + 0.1 * jax.random.normal(streams_of[12], (H, HD), jnp.float32), 0.5, 1.5).astype(jnp.bfloat16)
    mixed_shift = normal_values(streams_of[13], (H, HD), 0.2, 1.25, ((0, 2), (1, 4)))
    output_weight = normal_values(streams_of[14], (D, D), D ** -0.5, 0.21875, ((0, 2), (1, 4)))
    output_bias = normal_values(streams_of[15], (D,), 0.2, 1.25, ((0, 4),))
    second_gain = jnp.clip(1.0 + 0.1 * jax.random.normal(streams_of[16], (D,), jnp.float32), 0.5, 1.5).astype(jnp.bfloat16)
    second_shift = normal_values(streams_of[17], (D,), 0.2, 1.25, ((0, 4),))
    inner_weight = normal_values(streams_of[18], (D, FF), D ** -0.5, 0.21875, ((0, 4), (1, 2)))
    inner_bias = normal_values(streams_of[19], (FF // 128, 128), 0.5, 3.0, ((0, 2), (1, 4)))
    hidden_gain = jnp.clip(1.0 + 0.1 * jax.random.normal(streams_of[20], (FF // 128, 128), jnp.float32), 0.5, 1.5).astype(jnp.bfloat16)
    hidden_shift = normal_values(streams_of[21], (FF // 128, 128), 0.2, 1.25, ((0, 2), (1, 4)))
    outer_weight = normal_values(streams_of[22], (FF, D), FF ** -0.5, 0.109375, ((0, 2), (1, 4)))
    outer_bias = normal_values(streams_of[23], (D,), 0.2, 1.25, ((0, 4),))
    return {"inputs": inputs, "teacher": teacher, "segments": segments, "valid_mask": valid_mask, "offsets": offsets, "first_gain": first_gain, "first_shift": first_shift, "query_weight": query_weight, "key_weight": key_weight, "value_weight": value_weight, "query_bias": query_bias, "value_bias": value_bias, "mixed_gain": mixed_gain, "mixed_shift": mixed_shift, "output_weight": output_weight, "output_bias": output_bias, "second_gain": second_gain, "second_shift": second_shift, "inner_weight": inner_weight, "inner_bias": inner_bias, "hidden_gain": hidden_gain, "hidden_shift": hidden_shift, "outer_weight": outer_weight, "outer_bias": outer_bias}


EPS = 1e-05

@jax.custom_vjp
def low(v):
    return lax.optimization_barrier(v.astype(jnp.bfloat16)).astype(jnp.float32)

@jax.custom_vjp
def low_back(v):
    return v

def low_keep(v):
    return (low(v), None)

def low_pass(kept, grad):
    return (grad,)

def back_keep(v):
    return (v, None)

def back_low(kept, grad):
    return (low(grad),)
low.defvjp(low_keep, low_pass)
low_back.defvjp(back_keep, back_low)

def product(left, right):
    return jnp.dot(left, right, precision=lax.Precision.HIGHEST)

def plain_norm(values, gain_vec, shift_vec):
    centre = lax.optimization_barrier(jnp.mean(values, axis=-1, keepdims=True))
    centred = values - centre
    spread = lax.optimization_barrier(jnp.mean(centred * centred, axis=-1, keepdims=True))
    return centred * lax.rsqrt(spread + EPS) * gain_vec + shift_vec

def moment_norm(values, gain_vec, shift_vec):
    centre = lax.optimization_barrier(jnp.mean(values, axis=-1, keepdims=True))
    spread = lax.optimization_barrier(jnp.mean(values * values, axis=-1, keepdims=True)) - centre * centre
    return (values - centre) * lax.rsqrt(spread + EPS) * gain_vec + shift_vec

def multiplicity(segment, valid_mask, offset):
    positions = jnp.arange(SEQ, dtype=jnp.int32)
    row_pos = positions[:, None]
    col_pos = positions[None, :]
    allowed = (col_pos <= row_pos) & (segment[:, None] == segment[None, :]) & ((valid_mask[None, :] > 0) | (col_pos == row_pos))
    nearby = allowed & (row_pos // SEG == col_pos // SEG)
    dilated = allowed & ((row_pos - offset) % 2 == 0) & ((col_pos - offset) % 2 == 0)
    return nearby.astype(jnp.float32) + dilated.astype(jnp.float32)

def head_attention(queries, key_rows, value_rows, offset, segment, valid_mask):
    weight = multiplicity(segment, valid_mask, offset)
    scores = low_back(product(queries, key_rows.T) * HD ** (-0.5))
    exp_weight = low(weight * jnp.exp(scores))
    weighted = low_back(product(exp_weight, value_rows))
    denominator = lax.optimization_barrier(jnp.sum(exp_weight, axis=1, keepdims=True))
    return weighted / denominator

def sequence_layer(params, input_rows, segment, valid_mask, offsets):
    first_gain, first_shift, query_weight, key_weight, value_weight, query_bias, value_bias, mixed_gain, mixed_shift, output_weight, output_bias, second_gain, second_shift, inner_weight, inner_bias, hidden_gain, hidden_shift, outer_weight, outer_bias = params
    first_normed = low(plain_norm(input_rows, first_gain, first_shift))
    queries = low_back(low(product(first_normed, query_weight) + query_bias.reshape(-1)))
    key_rows = low_back(low(product(first_normed, key_weight)))
    value_rows = low_back(low(product(first_normed, value_weight) + value_bias.reshape(-1)))
    attend = jax.checkpoint(head_attention)

    def per_head(packed):
        return attend(packed[0], packed[1], packed[2], packed[3], segment, valid_mask)
    head_inputs = (queries.reshape(SEQ, H, HD).transpose(1, 0, 2), key_rows.reshape(SEQ, H, HD).transpose(1, 0, 2), value_rows.reshape(SEQ, H, HD).transpose(1, 0, 2), offsets)
    mixed_out = lax.map(per_head, head_inputs).transpose(1, 0, 2).reshape(SEQ, D)
    normed_mixed = low(moment_norm(mixed_out, mixed_gain.reshape(-1), mixed_shift.reshape(-1)))
    middle = input_rows + low_back(product(normed_mixed, output_weight)) + output_bias
    second_normed = low(plain_norm(middle, second_gain, second_shift))
    preact = low_back(product(second_normed, inner_weight) + inner_bias.reshape(-1))
    active = jax.nn.gelu(preact, approximate=False)
    normed_hidden = low(moment_norm(active, hidden_gain.reshape(-1), hidden_shift.reshape(-1)))
    return middle + low_back(product(normed_hidden, outer_weight)) + outer_bias

def reference(inputs, teacher, segments, valid_mask, offsets, first_gain, first_shift, query_weight, key_weight, value_weight, query_bias, value_bias, mixed_gain, mixed_shift, output_weight, output_bias, second_gain, second_shift, inner_weight, inner_bias, hidden_gain, hidden_shift, outer_weight, outer_bias):
    params = jax.tree.map(lambda weight_leaf: weight_leaf.astype(jnp.float32), (first_gain, first_shift, query_weight, key_weight, value_weight, query_bias, value_bias, mixed_gain, mixed_shift, output_weight, output_bias, second_gain, second_shift, inner_weight, inner_bias, hidden_gain, hidden_shift, outer_weight, outer_bias))
    input_rows = inputs.astype(jnp.float32)
    target = teacher.astype(jnp.float32)
    loss_mask = valid_mask.astype(jnp.float32)[:, :, None]
    token_count = jnp.sum(valid_mask).astype(jnp.float32)
    layer_fn = jax.checkpoint(sequence_layer)

    def objective(weights, source):

        def per_sequence(packed):
            return layer_fn(weights, packed[0], packed[1], packed[2], offsets)
        outputs = lax.map(per_sequence, (source, segments, valid_mask))
        difference = outputs - target
        loss = jnp.sum(loss_mask * difference * difference) / (2.0 * token_count * D)
        return (loss * (TOKENS * D), (outputs, loss))
    scaled, pullback, extras = jax.vjp(objective, params, input_rows, has_aux=True)
    weight_grads, input_grad = pullback(jnp.ones_like(scaled))
    outputs, loss = extras
    return (outputs.astype(jnp.bfloat16), loss, input_grad, weight_grads[0], weight_grads[1], weight_grads[2], weight_grads[3], weight_grads[4], weight_grads[5], weight_grads[6], weight_grads[7], weight_grads[8], weight_grads[9], weight_grads[10], weight_grads[11], weight_grads[12], weight_grads[13], weight_grads[14], weight_grads[15], weight_grads[16], weight_grads[17], weight_grads[18])
```

```python
import functools

import jax
import jax.numpy as jnp
from jax import lax
from jax.experimental import pallas as pl
from jax.experimental.pallas import tpu as pltpu
from jax.sharding import Mesh
from jax.sharding import PartitionSpec as P

EPS = 1e-05
F32 = jnp.float32
BF16 = jnp.bfloat16
DOCS = 8
TILE = 256
ROWS = 256
LANES = 128


def swap(values, axis):
    return lax.ppermute(values, axis, [(0, 1), (1, 0)])


def swap_diag(values, first, second):
    return lax.ppermute(values, (first, second), [(0, 3), (1, 2), (2, 1), (3, 0)])


def gather_shard(values):
    count = lax.axis_size("shard")
    if count > 8:
        return lax.all_gather(values, "shard", axis=0, tiled=False)
    here = lax.axis_index("shard")
    whole = jnp.zeros((count,) + values.shape, values.dtype)
    whole = lax.dynamic_update_index_in_dim(whole, values, here, 0)
    for step in range(1, count):
        came = lax.ppermute(values, "shard", [(i, (i + step) % count) for i in range(count)])
        whole = lax.dynamic_update_index_in_dim(whole, came, (here - step) % count, 0)
    return whole


def scatter_shard(values):
    count = lax.axis_size("shard")
    if count > 8:
        return lax.psum_scatter(values, "shard", scatter_dimension=0, tiled=False).astype(F32)
    here = lax.axis_index("shard")
    total = lax.dynamic_index_in_dim(values, here, 0, keepdims=False).astype(F32)
    for step in range(1, count):
        part = lax.dynamic_index_in_dim(values, (here + step) % count, 0, keepdims=False)
        came = lax.ppermute(part, "shard", [(i, (i + step) % count) for i in range(count)])
        total = total + came.astype(F32)
    return total


def butterfly(values, axis):
    count = lax.axis_size(axis)
    bit = 1
    while bit < count:
        values = values + lax.ppermute(values, axis, [(i, i ^ bit) for i in range(count)])
        bit *= 2
    return values


def doc_start(meta, position):
    start = position * 0
    for doc in range(1, DOCS):
        mark = meta[doc]
        start = jnp.where(position >= mark, jnp.maximum(start, mark), start)
    return start


def weight_tiles(meta, query_pos, key_pos, start, near):
    last = jnp.minimum(query_pos, meta[8] - 1)
    allowed = (key_pos >= start) & ((key_pos <= last) | (key_pos == query_pos))
    query_even = (1 - (query_pos & 1)).astype(F32)
    key_even = (1 - (key_pos & 1)).astype(F32)
    zero = jnp.zeros((), F32)
    even = jnp.where(allowed, near + query_even * key_even, zero)
    odd = jnp.where(allowed, near + (1.0 - query_even) * (1.0 - key_even), zero)
    return even, odd


def project_kernel(
    heads, size, meta, xa_ref, xb_ref, w_ref, b_ref, gain_ref, shift_ref, n_ref, q_ref, k_ref, v_ref
):
    rows = jnp.where(pl.program_id(0) == 0, xa_ref[...], xb_ref[...]).astype(F32)
    centred = rows - jnp.mean(rows, axis=-1, keepdims=True)
    inverse = lax.rsqrt(jnp.mean(centred * centred, axis=-1, keepdims=True) + EPS)
    normed = (centred * inverse * gain_ref[...] + shift_ref[...]).astype(BF16)
    n_ref[...] = normed
    out = jnp.dot(normed, w_ref[...], preferred_element_type=F32) + b_ref[...]
    count = rows.shape[0]
    width = heads * size
    zeros = jnp.zeros((count, LANES - size), BF16)
    lane = lax.broadcasted_iota(jnp.int32, (count, LANES - size), 1)
    ones = jnp.where(lane < 2, 1.0, 0.0).astype(BF16)
    scale = float(size) ** (-0.5)
    for head in range(heads):
        lo = head * size
        spot = slice(head * LANES, (head + 1) * LANES)
        query = (out[:, lo : lo + size].astype(BF16).astype(F32) * scale).astype(BF16)
        key = out[:, width + lo : width + lo + size].astype(BF16)
        value = out[:, 2 * width + lo : 2 * width + lo + size].astype(BF16)
        q_ref[:, spot] = jnp.concatenate([query, zeros], axis=1)
        k_ref[:, spot] = jnp.concatenate([key, zeros], axis=1)
        v_ref[:, spot] = jnp.concatenate([value, ones], axis=1)


def project(meta, mine, theirs, weight, bias, gain, shift, heads, size):
    rows, width = mine.shape
    steps = rows // ROWS
    ext = heads * LANES

    def out_map(block, step, meta):
        return (jnp.where(block == 0, meta[0], 1 - meta[0]) * steps + step, 0)

    def whole(*_):
        return (0, 0)

    return pl.pallas_call(
        functools.partial(project_kernel, heads, size),
        out_shape=[jax.ShapeDtypeStruct((2 * rows, width), BF16)]
        + [jax.ShapeDtypeStruct((2 * rows, ext), BF16)] * 3,
        grid_spec=pltpu.PrefetchScalarGridSpec(
            num_scalar_prefetch=1,
            grid=(2, steps),
            in_specs=[
                pl.BlockSpec((ROWS, width), lambda b, i, m: (jnp.where(b == 0, i, steps - 1), 0)),
                pl.BlockSpec((ROWS, width), lambda b, i, m: (jnp.where(b == 0, 0, i), 0)),
                pl.BlockSpec(weight.shape, whole),
                pl.BlockSpec(bias.shape, whole),
                pl.BlockSpec(gain.shape, whole),
                pl.BlockSpec(shift.shape, whole),
            ],
            out_specs=[pl.BlockSpec((ROWS, width), out_map)]
            + [pl.BlockSpec((ROWS, ext), out_map)] * 3,
        ),
        cost_estimate=pl.CostEstimate(
            flops=4 * rows * width * weight.shape[1], bytes_accessed=20_000_000, transcendentals=0
        ),
        name="project",
    )(meta, mine, theirs, weight, bias, gain, shift)


def attend_kernel(
    heads, size, half_len, meta, q_ref, ko_ref, vo_ref, kb_ref, vb_ref, m_ref, c_ref, acc_ref, w_ref
):
    step = pl.program_id(0)
    tall = q_ref.shape[0]
    chip_rows = ko_ref.shape[0]
    base = meta[9] * chip_rows
    first = base + step * tall
    query_pos = first + lax.broadcasted_iota(jnp.int32, (tall, 1), 0)
    start = doc_start(meta, query_pos)
    low = doc_start(meta, first)
    acc_ref[...] = jnp.zeros_like(acc_ref)

    def visit(k_ref, v_ref, key_base):
        def body(tile, carry):
            row = pl.multiple_of(tile * TILE, TILE)
            key_first = key_base + row
            key_pos = key_first + lax.broadcasted_iota(jnp.int32, (1, TILE), 1)
            near = jnp.where(first // half_len == key_first // half_len, 1.0, 0.0).astype(F32)
            even, odd = weight_tiles(meta, query_pos, key_pos, start, near)
            w_ref[0] = even
            w_ref[1] = odd
            for head in range(heads):
                spot = slice(head * LANES, (head + 1) * LANES)
                scores = lax.dot_general(
                    q_ref[:, spot],
                    k_ref[pl.ds(row, TILE), spot],
                    (((1,), (1,)), ((), ())),
                    preferred_element_type=F32,
                )
                exp_weight = (w_ref[meta[10 + head]] * jnp.exp(scores)).astype(BF16)
                acc_ref[:, spot] += jnp.dot(
                    exp_weight, v_ref[pl.ds(row, TILE), spot], preferred_element_type=F32
                )
            return carry

        return body

    crossing = (meta[9] > 0) & (low < base)
    other_low = jnp.where(crossing, low // TILE, 0)
    other_high = jnp.where(crossing, chip_rows // TILE, 0)
    lax.fori_loop(other_low, other_high, visit(kb_ref, vb_ref, 0), 0)
    own_low = jnp.maximum(low - base, 0) // TILE
    own_high = (step * tall + tall - 1) // TILE + 1
    lax.fori_loop(own_low, own_high, visit(ko_ref, vo_ref, base), 0)
    pieces = []
    lane = lax.broadcasted_iota(jnp.int32, (tall, LANES), 1)
    for head in range(heads):
        spot = slice(head * LANES, (head + 1) * LANES)
        total = acc_ref[:, spot]
        denominator = total[:, size : size + 1]
        mixed = total / denominator
        m_ref[:, spot] = jnp.where(lane < size, mixed, denominator)
        pieces.append(mixed[:, :size])
    c_ref[...] = jnp.concatenate(pieces, axis=1).astype(BF16)


def attend(meta, query, key, value, key_other, value_other, heads, size, half_len):
    rows, ext = query.shape
    full = pl.BlockSpec((rows, ext), lambda i, m: (0, 0))
    return pl.pallas_call(
        functools.partial(attend_kernel, heads, size, half_len),
        out_shape=[
            jax.ShapeDtypeStruct((rows, ext), F32),
            jax.ShapeDtypeStruct((rows, heads * size), BF16),
        ],
        grid_spec=pltpu.PrefetchScalarGridSpec(
            num_scalar_prefetch=1,
            grid=(rows // TILE,),
            in_specs=[pl.BlockSpec((TILE, ext), lambda i, m: (i, 0)), full, full, full, full],
            out_specs=[
                pl.BlockSpec((TILE, ext), lambda i, m: (i, 0)),
                pl.BlockSpec((TILE, heads * size), lambda i, m: (i, 0)),
            ],
            scratch_shapes=[pltpu.VMEM((TILE, ext), F32), pltpu.VMEM((2, TILE, TILE), F32)],
        ),
        cost_estimate=pl.CostEstimate(
            flops=20_000_000_000, bytes_accessed=16_000_000, transcendentals=6_000_000
        ),
        name="attend",
    )(meta, query, key, value, key_other, value_other)


def ready_kernel(heads, size, g_ref, m_ref, o_ref):
    grad = g_ref[...].astype(F32)
    rows = grad.shape[0]
    pieces, tails = [], []
    for head in range(heads):
        part = grad[:, head * size : (head + 1) * size]
        mixed = m_ref[:, head * LANES : head * LANES + size]
        denominator = m_ref[:, head * LANES + size : head * LANES + size + 1]
        pieces.append(part / denominator)
        term = -jnp.sum(part * mixed, axis=1, keepdims=True) / denominator
        high = term.astype(BF16).astype(F32)
        tails += [high, term - high]
    fill = jnp.zeros((rows, size - len(tails)), F32)
    o_ref[...] = jnp.concatenate(pieces + tails + [fill], axis=1).astype(BF16)


def ready(grad, mixed, heads, size):
    rows, width = grad.shape
    ext = mixed.shape[1]
    return pl.pallas_call(
        functools.partial(ready_kernel, heads, size),
        out_shape=jax.ShapeDtypeStruct((rows, width + size), BF16),
        grid=(rows // ROWS,),
        in_specs=[
            pl.BlockSpec((ROWS, width), lambda i: (i, 0)),
            pl.BlockSpec((ROWS, ext), lambda i: (i, 0)),
        ],
        out_specs=pl.BlockSpec((ROWS, width + size), lambda i: (i, 0)),
        cost_estimate=pl.CostEstimate(
            flops=rows * ext * 8, bytes_accessed=6_000_000, transcendentals=0
        ),
        name="ready",
    )(grad, mixed)


def back_kernel(
    heads, size, half_len, meta, q_ref, g_ref, k_ref, v_ref, dq_ref, dk_ref, dv_ref, w_ref, gw_ref
):
    step = pl.program_id(0)
    tall = q_ref.shape[0]
    key_rows = k_ref.shape[0]
    first = meta[9] + step * tall
    key_base = meta[13]
    low = doc_start(meta, first)

    @pl.when(step == 0)
    def _():
        dk_ref[...] = jnp.zeros_like(dk_ref)
        dv_ref[...] = jnp.zeros_like(dv_ref)

    dq_ref[...] = jnp.zeros_like(dq_ref)
    tile_low = jnp.maximum(low - key_base, 0) // TILE
    tile_high = jnp.minimum((first + tall - 1 - key_base) // TILE + 1, key_rows // TILE)
    query_pos = first + lax.broadcasted_iota(jnp.int32, (1, tall), 1)
    start = doc_start(meta, query_pos)
    fill = jnp.zeros((tall, LANES - size - 2), BF16)
    for head in range(heads):
        tail = heads * size + 2 * head
        gw_ref[:, head * LANES : (head + 1) * LANES] = jnp.concatenate(
            [g_ref[:, head * size : (head + 1) * size], g_ref[:, tail : tail + 2], fill], axis=1
        )

    def body(tile, carry):
        row = pl.multiple_of(tile * TILE, TILE)
        key_first = key_base + row
        key_pos = key_first + lax.broadcasted_iota(jnp.int32, (TILE, 1), 0)
        near = jnp.where(first // half_len == key_first // half_len, 1.0, 0.0).astype(F32)
        even, odd = weight_tiles(meta, query_pos, key_pos, start, near)
        w_ref[0] = even
        w_ref[1] = odd
        window = pl.ds(row, TILE)
        for head in range(heads):
            spot = slice(head * LANES, (head + 1) * LANES)
            key = k_ref[window, spot]
            across = (((1,), (1,)), ((), ()))
            scores = lax.dot_general(key, q_ref[:, spot], across, preferred_element_type=F32)
            grad_prob = lax.dot_general(
                v_ref[window, spot], gw_ref[:, spot], across, preferred_element_type=F32
            )
            exp_full = w_ref[meta[10 + head]] * jnp.exp(scores)
            exp_weight = exp_full.astype(BF16)
            grad_score = (exp_full * grad_prob).astype(BF16)
            dv_ref[window, spot] += jnp.dot(
                exp_weight, gw_ref[:, spot], preferred_element_type=F32
            )
            dk_ref[window, spot] += jnp.dot(
                grad_score, q_ref[:, spot], preferred_element_type=F32
            )
            dq_ref[:, spot] += lax.dot_general(
                grad_score, key, (((0,), (0,)), ((), ())), preferred_element_type=F32
            )
        return carry

    lax.fori_loop(tile_low, tile_high, body, 0)


def back(meta, query, grad, key, value, heads, size, half_len, name):
    rows, ext = query.shape
    full = pl.BlockSpec((rows, ext), lambda i, m: (0, 0))
    return pl.pallas_call(
        functools.partial(back_kernel, heads, size, half_len),
        out_shape=[jax.ShapeDtypeStruct((rows, ext), F32)] * 3,
        grid_spec=pltpu.PrefetchScalarGridSpec(
            num_scalar_prefetch=1,
            grid=(rows // TILE,),
            in_specs=[
                pl.BlockSpec((TILE, ext), lambda i, m: (i, 0)),
                pl.BlockSpec((TILE, grad.shape[1]), lambda i, m: (i, 0)),
                full,
                full,
            ],
            out_specs=[pl.BlockSpec((TILE, ext), lambda i, m: (i, 0)), full, full],
            scratch_shapes=[pltpu.VMEM((2, TILE, TILE), F32), pltpu.VMEM((TILE, ext), BF16)],
        ),
        cost_estimate=pl.CostEstimate(
            flops=30_000_000_000, bytes_accessed=20_000_000, transcendentals=6_000_000
        ),
        name=name,
    )(meta, query, grad, key, value)


def plain_stats(values):
    centre = jnp.mean(values, axis=-1, keepdims=True)
    centred = values - centre
    inverse = lax.rsqrt(jnp.mean(centred * centred, axis=-1, keepdims=True) + EPS)
    return centred * inverse, inverse


def moment_stats(values):
    centre = jnp.mean(values, axis=-1, keepdims=True)
    square = jnp.mean(values * values, axis=-1, keepdims=True)
    inverse = lax.rsqrt(square - centre * centre + EPS)
    return (values - centre) * inverse, inverse


def norm_back(grad_hat, normed, inverse):
    first_mean = jnp.mean(grad_hat, axis=-1, keepdims=True)
    second_mean = jnp.mean(grad_hat * normed, axis=-1, keepdims=True)
    return inverse * (grad_hat - first_mean - normed * second_mean)


def column_sum(values):
    return jnp.sum(values, axis=0, dtype=F32)


def gelu_exact(values):
    return jax.nn.gelu(values, approximate=False)


def pick(flag, first, second, axis):
    return jnp.where(
        flag == 0,
        jnp.concatenate([first, second], axis=axis),
        jnp.concatenate([second, first], axis=axis),
    )


def rows_of(values, index, count):
    return lax.dynamic_slice_in_dim(values, index * count, count, 0)


def columns_of(values, index, count):
    return lax.dynamic_slice_in_dim(values, index * count, count, 1)


def gather_rows(block):
    x, core = lax.axis_index("x"), lax.axis_index("core")
    rows, columns = block.shape
    quarter = lax.dynamic_index_in_dim(
        block.reshape(4, rows // 4, columns), 2 * x + core, 0, keepdims=False
    )
    mine = gather_shard(quarter)
    both = jnp.stack([mine, swap(mine, "tp")])
    both_x = swap(both, "x")
    both_c = swap(both, "core")
    both_xc = swap(both_x, "core")
    shards = mine.shape[0]
    whole = jnp.zeros((2, shards, 4, rows // 4, columns), block.dtype)
    spot = 2 * x + core
    for piece, place in ((both, spot), (both_x, spot ^ 2), (both_c, spot ^ 1), (both_xc, spot ^ 3)):
        whole = lax.dynamic_update_index_in_dim(whole, piece, place, 2)
    return whole.reshape(2, shards * rows, columns)


def reduce_rows(own, other):
    x, core = lax.axis_index("x"), lax.axis_index("core")
    shards = lax.axis_size("shard")
    rows, columns = own.shape
    fine = rows // shards // 4
    both = jnp.stack([own, other]).reshape(2, shards, 2, 2, fine, columns)
    keep = lax.dynamic_index_in_dim(both, core, 3, keepdims=False)
    send = lax.dynamic_index_in_dim(both, 1 - core, 3, keepdims=False)
    both = (keep.astype(F32) + swap(send, "core").astype(F32)).astype(BF16)
    keep = lax.dynamic_index_in_dim(both, x, 2, keepdims=False)
    send = lax.dynamic_index_in_dim(both, 1 - x, 2, keepdims=False)
    both = (keep.astype(F32) + swap(send, "x").astype(F32)).astype(BF16)
    half = (both[0].astype(F32) + swap(both[1], "tp").astype(F32)).astype(BF16)
    quarter = scatter_shard(half).astype(BF16)
    pair = pick(x, quarter[None], swap(quarter, "x")[None], 0)
    four = pick(core, pair[:, None], swap(pair, "core")[:, None], 1)
    return four.reshape(4 * fine, columns).astype(F32)


def on_device(
    inputs,
    teacher,
    segments,
    valid_mask,
    offsets,
    first_gain,
    first_shift,
    query_weight,
    key_weight,
    value_weight,
    query_bias,
    value_bias,
    mixed_gain,
    mixed_shift,
    output_weight,
    output_bias,
    second_gain,
    second_shift,
    inner_weight,
    inner_bias,
    hidden_gain,
    hidden_shift,
    outer_weight,
    outer_bias,
):
    _, block_len, width = inputs.shape
    shards = lax.axis_size("shard")
    z = lax.axis_index("shard")
    x = lax.axis_index("x")
    core = lax.axis_index("core")
    y = lax.axis_index("tp")
    chip_rows = 2 * block_len
    half_len = lax.axis_size("x") * lax.axis_size("core") * block_len // 2
    own_rows = block_len // 2
    heads = offsets.shape[0] // 2
    size = query_bias.shape[1] * shards
    group = heads * size
    units = inner_weight.shape[1]
    token_total = block_len * shards * lax.axis_size("x") * lax.axis_size("core")

    segment = segments.reshape(-1)
    tally = jnp.stack(
        [jnp.sum((segment < doc).astype(F32)) for doc in range(1, DOCS)]
        + [jnp.sum(valid_mask.astype(F32))]
    ).reshape(1, DOCS)
    tally = butterfly(butterfly(tally, "core"), "x")
    marks = tally.reshape(-1).astype(jnp.int32)
    token_count = butterfly(tally[:, DOCS - 1 :], "shard")[0, 0]
    here_offsets = lax.dynamic_slice_in_dim(offsets, core * heads, heads, 0)
    edge = jnp.stack([core, x]).astype(jnp.int32)
    meta = jnp.concatenate([edge[:1], marks, edge[1:], here_offsets, jnp.zeros((4,), jnp.int32)])

    def back_meta(query_base, key_base):
        ends = jnp.stack([jnp.asarray(query_base), jnp.asarray(key_base)]).astype(jnp.int32)
        return jnp.concatenate([edge[:1], marks, ends[:1], here_offsets, ends[1:]])

    block = inputs.reshape(block_len, width)
    block_c = swap(block, "core")
    block_x = swap(block, "x")
    block_xc = swap(block_x, "core")

    local = jnp.concatenate(
        [columns_of(w, core, group) for w in (query_weight, key_weight, value_weight)], axis=1
    )
    wide = gather_shard(local).reshape(width, 3 * group)
    zlist = (first_gain, first_shift, output_bias, second_gain, second_shift, outer_bias)
    hlist = (query_bias, value_bias, mixed_gain, mixed_shift)
    flist = (inner_bias, hidden_gain, hidden_shift)
    small = jnp.concatenate([v.reshape(-1) for v in zlist + hlist + flist]).reshape(1, -1)
    small = gather_shard(small).reshape(shards, -1)
    zlen = 6 * width // shards
    hlen = 4 * 2 * group // shards
    zpart = small[:, :zlen].reshape(shards, 6, -1).transpose(1, 0, 2).reshape(6, width)
    hpart = small[:, zlen : zlen + hlen].reshape(shards, 8 * heads, -1)
    hpart = hpart.transpose(1, 0, 2).reshape(4, 2 * group)
    fpart = small[:, zlen + hlen :].reshape(shards, 3 * inner_bias.shape[0], -1)
    fpart = fpart.transpose(1, 0, 2).reshape(3, units)
    far = swap(jnp.concatenate([hpart[2:].reshape(-1), fpart.reshape(-1)]).reshape(1, -1), "tp")
    far_h = far[0, : 4 * group].reshape(2, 2 * group)
    far_f = far[0, 4 * group :].reshape(3, units)
    zpart = zpart.astype(F32)
    mixed_rows = jnp.concatenate([hpart[2:], far_h], axis=1).astype(F32)
    unit_rows = jnp.concatenate([fpart, far_f], axis=1).astype(F32)
    bias_pair = columns_of(hpart[:2], core, group).astype(F32)
    bias = jnp.concatenate(
        [bias_pair[0], jnp.zeros((group,), F32), bias_pair[1]]
    ).reshape(1, 3 * group)
    gain_first, shift_first, bias_output, gain_second, shift_second, bias_outer = [
        zpart[i : i + 1] for i in range(6)
    ]
    gain_mixed, shift_mixed = mixed_rows[0:1], mixed_rows[1:2]
    bias_inner, gain_hidden, shift_hidden = [unit_rows[i : i + 1] for i in range(3)]

    first_pack = gather_rows(jnp.concatenate([output_weight.T, inner_weight], axis=1))
    wide_outer = gather_rows(outer_weight.T)
    wide_output = jnp.concatenate([first_pack[0, :, : 2 * group], first_pack[1, :, : 2 * group]], 1)
    wide_inner = jnp.concatenate([first_pack[0, :, 2 * group :], first_pack[1, :, 2 * group :]], 1)
    wide_outer = jnp.concatenate([wide_outer[0], wide_outer[1]], axis=1)

    first_normed, query, key, value = project(
        meta, block, block_c, wide, bias, gain_first, shift_first, heads, size
    )
    _, query_o, key_o, value_o = project(
        meta, block_x, block_xc, wide, bias, gain_first, shift_first, heads, size
    )
    mixed_ext, mixed_low = attend(
        meta, query, key, value, key_o, value_o, heads, size, half_len
    )

    parts = mixed_low.reshape(2, 2, own_rows, group)

    def part(c, h):
        return lax.dynamic_slice(parts, (c, h, 0, 0), (1, 1, own_rows, group))[0, 0]

    near_half = pick(core, part(core, y), swap(part(1 - core, y), "core"), 1)
    far_half = pick(
        core, swap(part(core, 1 - y), "tp"), swap_diag(part(1 - core, 1 - y), "core", "tp"), 1
    )
    mixed = jnp.concatenate([near_half, far_half], axis=1).astype(F32)

    source = rows_of(block, y, own_rows).astype(F32)
    hat_mixed, inverse_mixed = moment_stats(mixed)
    normed_mixed = (hat_mixed * gain_mixed + shift_mixed).astype(BF16)
    middle = (
        source
        + jnp.einsum("rf,df->rd", normed_mixed, wide_output, preferred_element_type=F32)
        + bias_output
    )
    norm_second, inverse_second = plain_stats(middle)
    second_normed = (norm_second * gain_second + shift_second).astype(BF16)
    preact = jnp.dot(second_normed, wide_inner, preferred_element_type=F32) + bias_inner
    active, gelu_pull = jax.vjp(gelu_exact, preact)
    hat_hidden, inverse_hidden = moment_stats(active)
    normed_hidden = (hat_hidden * gain_hidden + shift_hidden).astype(BF16)
    final_rows = (
        middle
        + jnp.einsum("rf,df->rd", normed_hidden, wide_outer, preferred_element_type=F32)
        + bias_outer
    )
    result_half = final_rows.astype(BF16)
    result = pick(y, result_half, swap(result_half, "tp"), 0)
    target = rows_of(teacher.reshape(block_len, width), y, own_rows).astype(F32)
    difference = final_rows - target
    loss_mask = rows_of(valid_mask.reshape(block_len, 1), y, own_rows).astype(F32)
    local_square = jnp.sum(loss_mask * difference * difference)
    grad_final = difference * loss_mask * (token_total / token_count)

    grad_bias_outer = column_sum(grad_final)
    grad_final_low = grad_final.astype(BF16)
    grad_wide_outer = jnp.einsum(
        "rd,rf->df", grad_final_low, normed_hidden, preferred_element_type=F32
    ).astype(BF16)
    grad_outer_shard = reduce_rows(grad_wide_outer[:, :units], grad_wide_outer[:, units:])
    grad_normed_hidden = jnp.dot(grad_final_low, wide_outer, preferred_element_type=F32)
    grad_gain_hidden = column_sum(grad_normed_hidden * hat_hidden)
    grad_shift_hidden = column_sum(grad_normed_hidden)
    grad_active = norm_back(grad_normed_hidden * gain_hidden, hat_hidden, inverse_hidden)
    grad_preact = gelu_pull(grad_active)[0].astype(BF16)
    grad_bias_inner = column_sum(grad_preact)
    grad_wide_inner = jnp.einsum(
        "rd,rf->df", second_normed, grad_preact, preferred_element_type=F32
    ).astype(BF16)
    grad_second_in = jnp.einsum("rf,df->rd", grad_preact, wide_inner, preferred_element_type=F32)
    grad_gain_second = column_sum(grad_second_in * norm_second)
    grad_shift_second = column_sum(grad_second_in)
    grad_middle = grad_final + norm_back(grad_second_in * gain_second, norm_second, inverse_second)
    grad_bias_output = column_sum(grad_middle)
    grad_middle_low = grad_middle.astype(BF16)
    grad_wide_output = jnp.einsum(
        "rd,rf->df", grad_middle_low, normed_mixed, preferred_element_type=F32
    ).astype(BF16)
    grad_rest_shard = reduce_rows(
        jnp.concatenate([grad_wide_output[:, : 2 * group], grad_wide_inner[:, :units]], axis=1),
        jnp.concatenate([grad_wide_output[:, 2 * group :], grad_wide_inner[:, units:]], axis=1),
    )
    grad_normed_mixed = jnp.dot(grad_middle_low, wide_output, preferred_element_type=F32)
    grad_gain_mixed = column_sum(grad_normed_mixed * hat_mixed)
    grad_shift_mixed = column_sum(grad_normed_mixed)
    grad_mixed = norm_back(grad_normed_mixed * gain_mixed, hat_mixed, inverse_mixed).astype(BF16)

    grad_near, grad_far = grad_mixed[:, : 2 * group], grad_mixed[:, 2 * group :]
    own_c = columns_of(grad_near, core, group)
    from_c = swap(columns_of(grad_near, 1 - core, group), "core")
    from_y = swap(columns_of(grad_far, core, group), "tp")
    from_cy = swap_diag(columns_of(grad_far, 1 - core, group), "core", "tp")
    grad_heads = pick(core, pick(y, own_c, from_y, 0), pick(y, from_c, from_cy, 0), 0)

    grad_pack = ready(grad_heads, mixed_ext, heads, size)
    grad_pack_x = swap(grad_pack, "x")
    own_base = x * chip_rows
    dq, dk, dv = back(
        back_meta(own_base, own_base), query, grad_pack, key, value, heads, size, half_len, "back_own"
    )
    late = x > 0
    cross = back(
        back_meta(jnp.int32(chip_rows), jnp.int32(0)),
        jnp.where(late, query, query_o),
        jnp.where(late, grad_pack, grad_pack_x),
        jnp.where(late, key_o, key),
        jnp.where(late, value_o, value),
        heads,
        size,
        half_len,
        "back_cross",
    )
    zero = jnp.zeros((), F32)
    dq = dq + jnp.where(late, cross[0], zero)
    dk = dk + jnp.where(late, zero, cross[1])
    dv = dv + jnp.where(late, zero, cross[2])

    def compact(values):
        return values.reshape(chip_rows, heads, LANES)[:, :, :size].reshape(chip_rows, group)

    grad_queries = (compact(dq) * (float(size) ** (-0.5))).astype(BF16)
    grad_keys = compact(dk).astype(BF16)
    grad_values = compact(dv).astype(BF16)
    grad_bias_query = column_sum(grad_queries)
    grad_bias_value = column_sum(grad_values)
    grad_three = jnp.concatenate([grad_queries, grad_keys, grad_values], axis=1)

    grad_wide = jnp.einsum(
        "rd,rf->df", first_normed, grad_three, preferred_element_type=F32
    ).astype(BF16)
    grad_wide = grad_wide.reshape(shards, 2, width // shards // 2, 3 * group)
    keep = lax.dynamic_index_in_dim(grad_wide, x, 1, keepdims=False)
    send = lax.dynamic_index_in_dim(grad_wide, 1 - x, 1, keepdims=False)
    grad_wide = (keep.astype(F32) + swap(send, "x").astype(F32)).astype(BF16)
    grad_piece = scatter_shard(grad_wide).astype(BF16)
    grad_piece = pick(x, grad_piece, swap(grad_piece, "x"), 0)
    grad_piece_c = swap(grad_piece, "core")
    projection_grads = [
        pick(
            core,
            grad_piece[:, i * group : (i + 1) * group],
            grad_piece_c[:, i * group : (i + 1) * group],
            1,
        ).astype(F32)
        for i in range(3)
    ]

    partial_first = jnp.einsum("rf,df->rd", grad_three, wide, preferred_element_type=F32)
    partial_block = rows_of(partial_first, core, block_len) + swap(
        rows_of(partial_first, 1 - core, block_len).astype(BF16), "core"
    ).astype(F32)
    grad_first_in = rows_of(partial_block, y, own_rows) + swap(
        rows_of(partial_block, 1 - y, own_rows).astype(BF16), "tp"
    ).astype(F32)
    norm_first, inverse_first = plain_stats(source)
    grad_gain_first = column_sum(grad_first_in * norm_first)
    grad_shift_first = column_sum(grad_first_in)
    input_half = (
        grad_middle + norm_back(grad_first_in * gain_first, norm_first, inverse_first)
    ).astype(BF16)
    input_grad = pick(y, input_half, swap(input_half, "tp"), 0).astype(F32)

    def absolute(values, length):
        return pick(y, values[:length], values[length:], 0)

    def placed(values):
        return lax.dynamic_update_slice_in_dim(
            jnp.zeros((width,), F32), values, (2 * y + core) * group, 0
        )

    pieces = [
        grad_gain_first,
        grad_shift_first,
        grad_bias_output,
        grad_gain_second,
        grad_shift_second,
        grad_bias_outer,
        placed(grad_bias_query),
        placed(grad_bias_value),
        absolute(grad_gain_mixed, 2 * group),
        absolute(grad_shift_mixed, 2 * group),
        absolute(grad_bias_inner, units),
        absolute(grad_gain_hidden, units),
        absolute(grad_shift_hidden, units),
        jnp.full((LANES,), local_square, F32),
    ]
    packed = jnp.concatenate(pieces).reshape(-1, LANES)
    for axis in ("core", "tp", "x", "shard"):
        packed = butterfly(packed, axis)
    packed = packed.reshape(-1)

    def model_slice(index):
        return lax.dynamic_slice_in_dim(
            packed, index * width + z * (width // shards), width // shards, 0
        )

    def head_slice(index):
        rows = packed[(6 + index) * width : (7 + index) * width].reshape(
            2, 2 * heads, shards, size // shards
        )
        return lax.dynamic_slice(
            rows, (y, 0, z, 0), (1, 2 * heads, 1, size // shards)
        ).reshape(2 * heads, size // shards)

    def unit_slice(index):
        begin = 10 * width + index * 2 * units
        rows = packed[begin : begin + 2 * units].reshape(
            2, inner_bias.shape[0], shards, inner_bias.shape[1]
        )
        return lax.dynamic_slice(
            rows, (y, 0, z, 0), (1, inner_bias.shape[0], 1, inner_bias.shape[1])
        ).reshape(inner_bias.shape)

    loss = packed[10 * width + 6 * units] / (2.0 * token_count * width)
    return (
        result.reshape(1, block_len, width),
        loss,
        input_grad.reshape(1, block_len, width),
        model_slice(0),
        model_slice(1),
        projection_grads[0],
        projection_grads[1],
        projection_grads[2],
        head_slice(0),
        head_slice(1),
        head_slice(2),
        head_slice(3),
        grad_rest_shard[:, : 2 * group].T,
        model_slice(2),
        model_slice(3),
        model_slice(4),
        grad_rest_shard[:, 2 * group :],
        unit_slice(0),
        unit_slice(1),
        unit_slice(2),
        grad_outer_shard.T,
        model_slice(5),
    )


def solution(mesh):
    shards, blocks, halves = mesh.devices.shape
    fine = Mesh(
        mesh.devices.reshape(shards, blocks // 2, 2, halves), ("shard", "x", "core", "tp")
    )
    rows = P("shard", ("x", "core"), None)
    flags = P("shard", ("x", "core"))
    return jax.shard_map(
        on_device,
        mesh=fine,
        in_specs=(
            rows,
            rows,
            flags,
            flags,
            P("tp"),
            P("shard"),
            P("shard"),
            P("shard", "tp"),
            P("shard", "tp"),
            P("shard", "tp"),
            P("tp", "shard"),
            P("tp", "shard"),
            P("tp", "shard"),
            P("tp", "shard"),
            P("tp", "shard"),
            P("shard"),
            P("shard"),
            P("shard"),
            P("shard", "tp"),
            P("tp", "shard"),
            P("tp", "shard"),
            P("tp", "shard"),
            P("tp", "shard"),
            P("shard"),
        ),
        out_specs=(
            rows,
            P(),
            rows,
            P("shard"),
            P("shard"),
            P("shard", "tp"),
            P("shard", "tp"),
            P("shard", "tp"),
            P("tp", "shard"),
            P("tp", "shard"),
            P("tp", "shard"),
            P("tp", "shard"),
            P("tp", "shard"),
            P("shard"),
            P("shard"),
            P("shard"),
            P("shard", "tp"),
            P("tp", "shard"),
            P("tp", "shard"),
            P("tp", "shard"),
            P("tp", "shard"),
            P("shard"),
        ),
        check_vma=False,
    )
```
